32 devices in a mesh: stn: 16 (over z, x, core), frq: 2 (over y).
Axes of the slice: x: 2, y: 2, z: 4, core: 2. Of those that a mesh axis runs over, the one named last changes fastest.
Arguments:
- spectra: bfloat16 [128, 2, 8192], P('stn', None, 'frq'), may hold values from -60 to 60, as said below
- pair_bin: int32 [4096, 1], P('stn'), may hold values from 0 to 15; in each aligned block of 256 rows (0 to 255, 256 to 511, ...) at most 34 rows name the same one
- pair_valid: int32 [4096], P('stn'), may hold values 0 or 1
- stack_in: float32 [16, 2048], P('stn', 'frq'), may hold values from -1.5 to 1.5
Outputs:
- stacks: float32 [16, 2048], P('stn', 'frq')
The draws below stay inside these ranges and needn't reach their ends.
Inputs may be any that keep to these rules, and one draw needn't show every extreme that they name: `spectra`: values have rough magnitudes, differing from bin to bin. `pair_bin`: in the 256 rows of one index of stn no bin is named more than 34 times.
All inputs are finite; a program needn't handle non-finite values. No bound on the sum of `pair_valid` on one device may be relied on, other than what follows from the above.
Results may differ from the reference program's by a relative error of at most 0.008.
Values may be sent and summed in bfloat16 or wider, within the bound.
No kernel may reach another device: no remote copies, remote signals or barrier semaphores. Data moves between devices by JAX's collectives and lax.ppermute only.
A program may use at most 64 MiB of HBM per device.

```python
import math
import jax
import jax.numpy as jnp
import numpy as np
from jax import lax

STN_DEV = 8
ROUNDS = 4
FREQ = 8192
SAMPLES = 32768
LAGS = 2048
WBLK = 32
STATIONS = 128
PAIRS_DEV = 256
PAIRS = 4096
BINS = 16
CAP = 34
N_STN = 16


def draw_spectra(key, part):
    shape = (STATIONS, 2, FREQ)
    first, second = jax.random.split(key, 2)
    base = jax.random.truncated_normal(first, -6.0, 6.0, shape, jnp.float32)
    factor = jnp.exp(jax.random.uniform(second, shape, jnp.float32, 0.0, math.log(10.0)))
    return (base * factor).astype(jnp.bfloat16)


def set_ends(drawn, stream_key, least, high):
    index_at = [jax.random.randint(jax.random.fold_in(stream_key, axis), (), 0, length) for axis, length in enumerate(drawn.shape)]
    longest = drawn.shape.index(max(drawn.shape))
    beside = index_at[:longest] + [(index_at[longest] + 1) % drawn.shape[longest]] + index_at[longest + 1:]
    return drawn.at[tuple(index_at)].set(least).at[tuple(beside)].set(high)


def steps_of(stream_key, dims, cuts, least, largest):
    gain, own = 1.0, jax.random.fold_in(stream_key, 6)
    for axis_at, blocks in cuts:
        heights = jnp.exp(jax.random.uniform(jax.random.fold_in(own, axis_at), (blocks,), jnp.float32, least / len(cuts), largest / len(cuts)))
        gain = gain * jnp.repeat(heights, dims[axis_at] // blocks).reshape([-1 if axis == axis_at else 1 for axis in range(len(dims))])
    return gain


def routed_block(stream_key, own, number, rows, count, top, reach, slope):
    ranking = jax.random.permutation(stream_key, count)
    crowded, usual = load_shares(count, rows * top, reach, slope, True), load_shares(count, rows * top, reach, slope, False)
    places = jnp.arange(count)

    def named(lengths, turn):
        used = int((lengths > 0).sum())
        fixed = max(1, used // 4)
        shifted = fixed + (places - fixed + turn * (used - fixed)) % max(1, count - fixed)
        return jnp.zeros((count,), jnp.int32).at[ranking[jnp.where(places < fixed, places, shifted)]].set(jnp.asarray(lengths, jnp.int32))

    lengths = jnp.where(number % 4 == 0, named(crowded, number // 4), named(usual, number - number // 4 - 1))
    mixed = jax.random.permutation(jax.random.fold_in(own, 3), count)
    donor, receiver = mixed[0:count // 2 * 2:2], mixed[1:count // 2 * 2:2]
    room = jnp.minimum(lengths[donor] - 1, reach - lengths[receiver]) // 2
    room = jnp.where((donor == ranking[0]) | (receiver == ranking[0]) | (lengths[receiver] == 0), 0, jnp.maximum(room, 0))
    shifted = jax.random.randint(jax.random.fold_in(own, 4), (count // 2,), 0, 1 << 20) % (room + 1)
    lengths = lengths.at[donor].add(-shifted).at[receiver].add(shifted)
    members = jnp.searchsorted(jnp.cumsum(lengths), jnp.arange(rows * top), side="right").astype(jnp.int32)
    grid = members.reshape(top, rows).T
    grid = grid[jax.random.permutation(jax.random.fold_in(own, 1), rows)]
    turn = jax.random.randint(jax.random.fold_in(own, 2), (rows, 1), 0, top)
    return jnp.take_along_axis(grid, (jnp.arange(top)[None, :] + turn) % top, axis=1)


def load_shares(amount, total, limit, lean, full):
    weights = [(1 << 20) // math.isqrt(rank ** lean) + 1 for rank in range(1, amount + 1)]
    largest = limit if full else min(limit, max(-(-total // amount), total * weights[0] // sum(weights)))
    least = 1 if total - largest >= amount - 1 else 0
    holding, surplus = [largest] + [least] * (amount - 1), total - largest - least * (amount - 1)
    while surplus > 0:
        candidates = [i for i in range(1, amount) if holding[i] < largest] or [i for i in range(1, amount) if holding[i] < limit]
        pool, budget = sum([weights[i] for i in candidates]), surplus
        for i in candidates:
            addition = min(limit - holding[i], max(1, budget * weights[i] // pool), surplus)
            holding[i] = holding[i] + addition
            surplus = surplus - addition
    return np.array(holding)


def noise(key, dims, deviation, reach, cuts=(), kind=jnp.bfloat16):
    entries = deviation * jax.random.normal(key, dims, jnp.float32)
    if cuts:
        entries = entries * steps_of(key, dims, cuts, -0.22, 0.18)
    return jnp.clip(entries, -reach, reach).astype(kind)


def setup_inputs(seed: int = 0) -> dict:
    key_list = jax.random.split(jax.random.key(seed), 5)
    spectra = draw_spectra(jax.random.fold_in(key_list[4], 71), 0)
    pair_bin_keys = jax.random.split(jax.random.fold_in(key_list[1], 1), PAIRS // PAIRS_DEV)
    pair_bin_turns = jax.random.permutation(jax.random.fold_in(key_list[1], 3), PAIRS // PAIRS_DEV)
    pair_bin = jax.vmap(lambda own, number: routed_block(jax.random.fold_in(key_list[1], 2), own, number, PAIRS_DEV, BINS, 1, CAP, 2))(pair_bin_keys, pair_bin_turns).reshape((PAIRS, 1))
    pair_valid = set_ends((jax.random.randint(key_list[2], (PAIRS,), 0, 4) < 3).astype(jnp.int32), jax.random.fold_in(key_list[2], 1), 0, 1)
    stack_in = noise(key_list[3], (BINS, LAGS), 0.1, 1.5, ((0, 16), (1, 2)), jnp.float32)
    return {"spectra": spectra, "pair_bin": pair_bin, "pair_valid": pair_valid, "stack_in": stack_in}


def whiten(spectra, count):
    values = spectra.astype(jnp.float32)
    blocks = values.reshape(count, 2, FREQ // WBLK, WBLK)
    power = lax.optimization_barrier(jnp.mean(blocks * blocks, axis=(1, 3), keepdims=True))
    return (blocks / jnp.sqrt(power + 1e-06)).reshape(count, 2, FREQ).astype(jnp.bfloat16)

def cross_block(own, partner):
    own_f = own.astype(jnp.float32)
    part_f = partner.astype(jnp.float32)
    real_part = own_f[:, 0][:, None, :] * part_f[:, 0][None] + own_f[:, 1][:, None, :] * part_f[:, 1][None]
    imag_part = own_f[:, 1][:, None, :] * part_f[:, 0][None] - own_f[:, 0][:, None, :] * part_f[:, 1][None]
    joined = jnp.concatenate([real_part, imag_part], axis=2)
    return joined.reshape(own.shape[0] * partner.shape[0], -1).astype(jnp.bfloat16)

def reference(spectra, pair_bin, pair_valid, stack_in):
    white = whiten(spectra, STATIONS)
    freq_index = 1 + jnp.arange(FREQ, dtype=jnp.int32)
    lag_index = jnp.arange(LAGS, dtype=jnp.int32) - LAGS // 2
    product = freq_index[:, None] * lag_index[None, :] % SAMPLES
    angle = product.astype(jnp.float32) * (2.0 * math.pi / SAMPLES)
    table = jnp.concatenate([jnp.cos(angle), -jnp.sin(angle)], axis=0).astype(jnp.bfloat16)
    grouped = white.reshape(N_STN, STN_DEV, 2, FREQ)
    bin_ids = jnp.arange(BINS, dtype=jnp.int32)

    def per_device(totals, device):
        own = grouped[device]
        pieces = []
        for turn in range(ROUNDS):
            source = ((device - turn - 1) % N_STN).astype(jnp.int32)
            pieces.append(cross_block(own, grouped[source]))
        cross_all = jnp.concatenate(pieces, axis=0)
        corr = jnp.dot(cross_all, table, preferred_element_type=jnp.float32) * (1.0 / FREQ)
        start = (device * PAIRS_DEV).astype(jnp.int32)
        valid = lax.dynamic_slice_in_dim(pair_valid, start, PAIRS_DEV, 0).astype(jnp.float32)
        bins = lax.dynamic_slice_in_dim(pair_bin[:, 0], start, PAIRS_DEV, 0)
        weighted = corr * valid[:, None]
        onehot = (bins[:, None] == bin_ids[None, :]).astype(jnp.float32)
        sums = jnp.dot(onehot.T, weighted, precision=lax.Precision.HIGHEST, preferred_element_type=jnp.float32)
        return (totals + sums, None)
    totals, unused = lax.scan(per_device, jnp.zeros((BINS, LAGS), jnp.float32), jnp.arange(N_STN, dtype=jnp.int32))
    return stack_in + totals
```

```python
import functools
import math

import jax
import jax.numpy as jnp
from jax import lax
from jax.experimental import pallas as pl
from jax.experimental.pallas import tpu as pltpu
from jax.sharding import PartitionSpec as P

ROUNDS = 4
SAMPLES = 32768
WBLK = 32
LANES = 128


def whiten_band(spectra):
    count, _, width = spectra.shape
    values = spectra.astype(jnp.float32)
    blocks = values.reshape(count, 2, width // WBLK, WBLK)
    power = jnp.mean(blocks * blocks, axis=(1, 3), keepdims=True)
    return (blocks / jnp.sqrt(power + 1e-06)).reshape(count, 2, width).astype(jnp.bfloat16)


def code_rows(pair_bin, pair_valid, own, owners, block):
    codes = jnp.where(pair_valid != 0, pair_bin[:, 0] + 1, 0).astype(jnp.float32)
    rows = codes.reshape(ROUNDS, block, block).transpose(1, 0, 2)
    place = lax.iota(jnp.int32, owners)[None, :]
    source = (own - 1 - lax.iota(jnp.int32, ROUNDS)[:, None]) % owners
    chosen = (place == source).astype(jnp.float32)
    return jnp.einsum("irj,rd->idj", rows, chosen, precision=lax.Precision.HIGHEST).reshape(
        block, owners * block
    )


def bin_kernel(owners, copies, block, halves, got_ref, sums_ref):
    stations = owners * block
    lanes = got_ref.shape[2]
    tile = lambda place: got_ref[:, place * block : (place + 1) * block, :].reshape(stations, lanes)
    pieces = [tile(place) for place in range(2 * halves)]
    codes = [tile(2 * halves + place) for place in range(stations // lanes)]
    codes = jnp.concatenate(codes, axis=1).astype(jnp.float32)
    right = jnp.concatenate(pieces, axis=1)
    left = [piece.astype(jnp.float32) for piece in pieces]
    for owner in range(owners):
        chosen = jnp.where(codes == float(owner + 1), 1.0, 0.0).astype(jnp.bfloat16)
        mixed = jnp.dot(chosen, right, preferred_element_type=jnp.float32)
        for half in range(halves):
            own_re, own_im = left[2 * half], left[2 * half + 1]
            mix_re = mixed[:, 2 * half * lanes : (2 * half + 1) * lanes]
            mix_im = mixed[:, (2 * half + 1) * lanes : (2 * half + 2) * lanes]
            real = jnp.sum(own_re * mix_re + own_im * mix_im, axis=0, keepdims=True)
            imag = jnp.sum(own_im * mix_re - own_re * mix_im, axis=0, keepdims=True)
            for copy in range(copies):
                place = owner * copies + copy
                sums_ref[place, half : half + 1, :] = real
                sums_ref[place, halves + half : halves + half + 1, :] = imag


def turn(product, period):
    angle = lax.rem(product, jnp.int32(period)).astype(jnp.float32) * (2.0 * math.pi / period)
    return jnp.cos(angle), jnp.sin(angle)


def iota(shape, dimension):
    return lax.broadcasted_iota(jnp.int32, shape, dimension)


def lag_kernel(owners, bands, halves, scale, band_ref, sums_ref, stack_ref, out_ref):
    sources = owners * bands
    fine = halves * sums_ref.shape[2]
    coarse = SAMPLES // fine
    turns = out_ref.shape[1] // coarse
    exact = lax.Precision.HIGHEST
    part = lambda row: sums_ref[:, row, :]
    real = jnp.concatenate([part(half) for half in range(halves)], axis=1)
    imag = jnp.concatenate([part(halves + half) for half in range(halves)], axis=1)
    shape = (coarse, sources)
    source = iota(shape, 1)
    upper = lax.rem(source, jnp.int32(bands)) * owners + lax.div(source, jnp.int32(bands))
    cos1, sin1 = turn(upper * iota(shape, 0), coarse)
    first = jnp.concatenate(
        [jnp.concatenate([cos1, -sin1], axis=1), jnp.concatenate([sin1, cos1], axis=1)], axis=0
    )
    mixed = jnp.dot(
        first, jnp.concatenate([real, imag], axis=0), precision=exact, preferred_element_type=jnp.float32
    )
    shape = (coarse, fine)
    cos2, sin2 = turn((iota(shape, 1) + 1) * iota(shape, 0), SAMPLES)
    mix_re, mix_im = mixed[:coarse], mixed[coarse:]
    turned = jnp.concatenate([mix_re * cos2 - mix_im * sin2, mix_re * sin2 + mix_im * cos2], axis=1)
    shape = (turns, fine)
    step = iota(shape, 0) + band_ref[0] * turns + (SAMPLES - bands * turns // 2)
    cos3, sin3 = turn((iota(shape, 1) + 1) * step, fine)
    last = jnp.concatenate([cos3, -sin3], axis=1)
    lags = lax.dot_general(
        last, turned, (((1,), (1,)), ((), ())), precision=exact, preferred_element_type=jnp.float32
    )
    for row in range(turns):
        place = slice(row * coarse, (row + 1) * coarse)
        out_ref[:, place] = stack_ref[:, place] + lags[row : row + 1, :] * scale


def whole(memory=pltpu.VMEM):
    return pl.BlockSpec(memory_space=memory)


def local(spectra, pair_bin, pair_valid, stack_in):
    block, _, width = spectra.shape
    owners, bands = lax.axis_size("stn"), lax.axis_size("frq")
    own, band = lax.axis_index("stn"), lax.axis_index("frq")
    fine = width // owners
    lanes = min(fine, LANES)
    halves = fine // lanes
    white = whiten_band(spectra)
    tiles = white.reshape(block, 2, owners, halves, lanes).transpose(2, 3, 1, 0, 4)
    tiles = tiles.reshape(owners, halves * 2 * block, lanes)
    codes = code_rows(pair_bin, pair_valid, own, owners, block).astype(jnp.bfloat16)
    codes = codes.reshape(block, -1, lanes).transpose(1, 0, 2).reshape(-1, lanes)
    codes = jnp.broadcast_to(codes[None], (owners,) + codes.shape)
    got = lax.all_to_all(jnp.concatenate([tiles, codes], axis=1), "stn", 0, 0, tiled=True)
    sums = pl.pallas_call(
        functools.partial(bin_kernel, owners, bands, block, halves),
        out_shape=jax.ShapeDtypeStruct((owners * bands, 2 * halves, lanes), jnp.float32),
        in_specs=[whole()],
        out_specs=whole(),
    )(got)
    sums = lax.all_to_all(sums, ("stn", "frq"), 0, 0, tiled=True)
    return pl.pallas_call(
        functools.partial(lag_kernel, owners, bands, halves, 1.0 / (width * bands)),
        out_shape=jax.ShapeDtypeStruct(stack_in.shape, jnp.float32),
        in_specs=[whole(pltpu.SMEM), whole(), whole()],
        out_specs=whole(),
    )(band[None], sums, stack_in)


def solution(mesh):
    placed = (P("stn", None, "frq"), P("stn", None), P("stn"), P("stn", "frq"))
    return jax.shard_map(
        local, mesh=mesh, in_specs=placed, out_specs=P("stn", "frq"), check_vma=False
    )
```

```python
import functools
import math

import jax
import jax.numpy as jnp
from jax import lax
from jax.experimental import pallas as pl
from jax.experimental.pallas import tpu as pltpu
from jax.sharding import PartitionSpec as P

ROUNDS = 4
SAMPLES = 32768
WBLK = 32
LANES = 128
TILE = 8


def iota(shape, dimension):
    return lax.broadcasted_iota(jnp.int32, shape, dimension)


def split(value):
    upper = value.astype(jnp.bfloat16)
    return upper, (value - upper.astype(jnp.float32)).astype(jnp.bfloat16)


def dot(left, right):
    return jnp.dot(left, right, preferred_element_type=jnp.float32)


def pack_kernel(owners, bands, block, scale, spectra_ref, bin_ref, valid_ref, stack_ref, *refs):
    pack_ref, held_ref, *tables, bins, valids, sems = refs
    stations = owners * block
    pairs = bins.shape[1]
    lanes = pack_ref.shape[3]
    copies = [
        pltpu.make_async_copy(bin_ref, bins, sems.at[0]),
        pltpu.make_async_copy(valid_ref, valids, sems.at[1]),
        pltpu.make_async_copy(stack_ref, held_ref, sems.at[2]),
    ]
    tiles = pack_ref.shape[1] - stations // lanes * (block // 2)
    if len(spectra_ref.shape) == 3:
        halves = tiles // block
        for place in range(owners * halves):
            source = spectra_ref.at[:, :, pl.ds(place * lanes, lanes)]
            target = pack_ref.at[place // halves, pl.ds(place % halves * block, block)]
            copies.append(pltpu.make_async_copy(source, target, sems.at[3 + place]))
    else:
        target = pack_ref.at[:, pl.ds(0, tiles)]
        copies.append(pltpu.make_async_copy(spectra_ref, target, sems.at[3]))
    for copy in copies:
        copy.start()
    place = iota((block, pairs), 1)
    mine = lax.rem(lax.div(place, block), block) == iota((block, pairs), 0)
    place = iota((pairs, stations), 0)
    ahead = lax.axis_index("stn") + (owners - 1)
    other = lax.rem(ahead - lax.div(place, block * block), owners) * block + lax.rem(place, block)
    right = jnp.where(other == iota((pairs, stations), 1), 1.0, 0.0).astype(jnp.bfloat16)
    fill_tables(owners, bands, scale, *tables)
    copies[0].wait()
    copies[1].wait()
    codes = jnp.where(valids[...] != 0, bins[...] + 1, 0).astype(jnp.float32)
    left = jnp.where(mine, jnp.broadcast_to(codes, (block, pairs)), 0.0).astype(jnp.bfloat16)
    codes = dot(left, right)
    for place in range(stations // lanes):
        piece = codes[:, place * lanes : (place + 1) * lanes].reshape(block // 2, 2, lanes)
        piece = piece.astype(jnp.bfloat16)
        start = tiles + place * (block // 2)
        for owner in range(owners):
            pack_ref[owner, start : start + block // 2] = piece
    for copy in copies[2:]:
        copy.wait()


def bin_kernel(owners, copies, block, halves, got_ref, sums_ref, rows_ref):
    stations = owners * block
    lanes = got_ref.shape[2]
    start = 2 * halves * block
    codes = [
        got_ref[:, start + place * block : start + (place + 1) * block, :].reshape(stations, lanes)
        for place in range(stations // lanes)
    ]
    codes = jnp.concatenate(codes, axis=1).astype(jnp.float32)
    shape = (lanes, lanes)
    same = lax.div(iota(shape, 0), WBLK) == lax.div(iota(shape, 1), WBLK)
    same = jnp.where(same, 0.5 / WBLK, 0.0).astype(jnp.bfloat16)
    pieces = []
    for half in range(halves):
        raw = got_ref[:, 2 * half * block : 2 * (half + 1) * block, :].astype(jnp.float32)
        rows_ref[half] = raw.reshape(2 * stations, lanes)
        raw = [rows_ref[half, pl.ds(part, stations, stride=2), :] for part in range(2)]
        upper, lower = split(raw[0] * raw[0] + raw[1] * raw[1])
        scale = lax.rsqrt(dot(upper, same) + dot(lower, same) + 1e-06)
        pieces += [(value * scale).astype(jnp.bfloat16) for value in raw]
    right = jnp.concatenate(pieces, axis=1)
    left = [piece.astype(jnp.float32) for piece in pieces]
    for owner in range(owners):
        chosen = jnp.where(codes == float(owner + 1), 1.0, 0.0).astype(jnp.bfloat16)
        mixed = dot(chosen, right)
        for half in range(halves):
            own_re, own_im = left[2 * half], left[2 * half + 1]
            mix_re = mixed[:, 2 * half * lanes : (2 * half + 1) * lanes]
            mix_im = mixed[:, (2 * half + 1) * lanes : (2 * half + 2) * lanes]
            real = jnp.sum(own_re * mix_re + own_im * mix_im, axis=0, keepdims=True)
            imag = jnp.sum(own_im * mix_re - own_re * mix_im, axis=0, keepdims=True)
            for copy in range(copies):
                place = owner * copies + copy
                sums_ref[place, half : half + 1, :] = real
                sums_ref[place, halves + half : halves + half + 1, :] = imag


def turn(product, period, ahead=0.0):
    angle = lax.rem(product, jnp.int32(period)).astype(jnp.float32) * (2.0 * math.pi / period) + ahead
    return jnp.cos(angle), jnp.sin(angle)


def powers(factor, period, count, store, ahead=0.0):
    width = factor.shape[1]
    near_cos, near_sin = turn(factor * iota((TILE, width), 0), period, ahead)
    far_cos, far_sin = turn(factor * (TILE * iota((count // TILE, width), 0)), period)
    for step in range(count // TILE):
        cos, sin = far_cos[step : step + 1, :], far_sin[step : step + 1, :]
        store(step * TILE, near_cos * cos - near_sin * sin, near_sin * cos + near_cos * sin)


def fill_tables(owners, bands, scale, first_ref, turn_ref, last_ref):
    coarse, span = first_ref.shape[0] // 2, first_ref.shape[1] // 3
    turns, fine = last_ref.shape[0] // 2, last_ref.shape[1] // 2

    width = max(span, LANES)
    column = lax.rem(iota((1, width), 1), span)
    source = lax.rem(column, owners * bands)
    factor = lax.rem(source, bands) * owners + lax.div(source, bands)
    ahead = jnp.where(column < owners * bands, 0.0, 0.5 * math.pi)

    def store_first(start, cos, sin):
        for begin, value in ((start, cos), (coarse + start, sin)):
            upper, lower = split(value)
            for place in range(0, 2 * span, width):
                first_ref[begin : begin + TILE, place : place + width] = upper
            first_ref[begin : begin + TILE, 2 * span :] = lower[:, :span]

    def store_turn(start, cos, sin):
        turn_ref[start : start + TILE, :] = cos
        turn_ref[coarse + start : coarse + start + TILE, :] = sin

    powers(factor, coarse, coarse, store_first, ahead)
    powers(iota((1, fine), 1) + 1, SAMPLES, coarse, store_turn)
    shape = (turns, fine)
    band = lax.axis_index("frq")
    step = iota(shape, 0) + band * turns + (SAMPLES - bands * turns // 2)
    cos, sin = turn((iota(shape, 1) + 1) * step, fine)
    upper, lower = split(jnp.concatenate([cos, -sin], axis=1) * scale)
    last_ref[...] = jnp.concatenate([upper, lower], axis=0)


def lag_kernel(halves, first_ref, turn_ref, last_ref, sums_ref, stack_ref, out_ref):
    coarse = first_ref.shape[0] // 2
    turns = last_ref.shape[0] // 2
    part = lambda row: sums_ref[:, row, :]
    real = jnp.concatenate([part(half) for half in range(halves)], axis=1)
    imag = jnp.concatenate([part(halves + half) for half in range(halves)], axis=1)
    upper, lower = split(jnp.concatenate([real, imag], axis=0))
    mixed = dot(first_ref[...], jnp.concatenate([upper, lower, upper], axis=0))
    mix_re, mix_im = mixed[:coarse], mixed[coarse:]
    cos, sin = turn_ref[:coarse, :], turn_ref[coarse:, :]
    turned = jnp.concatenate([mix_re * cos - mix_im * sin, mix_re * sin + mix_im * cos], axis=1)
    upper, lower = split(turned)
    across = lambda left, right: lax.dot_general(
        left, right, (((1,), (1,)), ((), ())), preferred_element_type=jnp.float32
    )
    lags = across(last_ref[...], upper)
    lags = lags[:turns] + lags[turns:] + across(last_ref[:turns, :], lower)
    for row in range(turns):
        place = slice(row * coarse, (row + 1) * coarse)
        out_ref[:, place] = stack_ref[:, place] + lags[row : row + 1, :]


def whole(memory=pltpu.VMEM):
    return pl.BlockSpec(memory_space=memory)


def near(value):
    return pltpu.with_memory_space_constraint(value, pltpu.VMEM)


def local(spectra, pair_bin, pair_valid, stack_in):
    block, _, width = spectra.shape
    owners, bands = lax.axis_size("stn"), lax.axis_size("frq")
    stations = owners * block
    pairs = pair_valid.shape[0]
    fine = width // owners
    lanes = min(fine, LANES)
    halves = fine // lanes
    coarse = SAMPLES // fine
    turns = stack_in.shape[1] // coarse
    if lanes < LANES:
        spectra = spectra.reshape(block, 2, owners, halves, lanes).transpose(2, 3, 0, 1, 4)
        spectra = spectra.reshape(owners, halves * block, 2, lanes)
    rows = halves * block + stations // lanes * (block // 2)
    packed, stack, *tables = pl.pallas_call(
        functools.partial(pack_kernel, owners, bands, block, 1.0 / (width * bands)),
        out_shape=[
            pltpu.VMEM((owners, rows, 2, lanes), jnp.bfloat16),
            pltpu.VMEM(stack_in.shape, jnp.float32),
            pltpu.VMEM((2 * coarse, 6 * owners * bands), jnp.bfloat16),
            pltpu.VMEM((2 * coarse, fine), jnp.float32),
            pltpu.VMEM((2 * turns, 2 * fine), jnp.bfloat16),
        ],
        in_specs=[whole(pl.ANY)] * 4,
        out_specs=[whole()] * 5,
        scratch_shapes=[
            pltpu.VMEM((1, pairs), jnp.int32),
            pltpu.VMEM((1, pairs), jnp.int32),
            pltpu.SemaphoreType.DMA((3 + owners * halves,)),
        ],
    )(spectra, pair_bin.reshape(1, pairs), pair_valid.reshape(1, pairs), stack_in)
    got = lax.all_to_all(packed.reshape(owners, 2 * rows, lanes), "stn", 0, 0, tiled=True)
    sums = pl.pallas_call(
        functools.partial(bin_kernel, owners, bands, block, halves),
        out_shape=pltpu.VMEM((owners * bands, 2 * halves, lanes), jnp.float32),
        in_specs=[whole()],
        out_specs=whole(),
        scratch_shapes=[pltpu.VMEM((halves, 2 * stations, lanes), jnp.float32)],
    )(near(got))
    sums = lax.all_to_all(sums, ("stn", "frq"), 0, 0, tiled=True)
    return pl.pallas_call(
        functools.partial(lag_kernel, halves),
        out_shape=jax.ShapeDtypeStruct(stack_in.shape, jnp.float32),
        in_specs=[whole()] * 5,
        out_specs=whole(),
    )(*[near(value) for value in (*tables, sums, stack)])


def solution(mesh):
    placed = (P("stn", None, "frq"), P("stn", None), P("stn"), P("stn", "frq"))
    return jax.shard_map(
        local, mesh=mesh, in_specs=placed, out_specs=P("stn", "frq"), check_vma=False
    )
```

```python
import functools
import math

import jax
import jax.numpy as jnp
from jax import lax
from jax.experimental import pallas as pl
from jax.experimental.pallas import tpu as pltpu
from jax.sharding import PartitionSpec as P

ROUNDS = 4
SAMPLES = 32768
WBLK = 32
LANES = 128
TILE = 8


def iota(shape, dimension):
    return lax.broadcasted_iota(jnp.int32, shape, dimension)


def split(value):
    upper = value.astype(jnp.bfloat16)
    return upper, (value - upper.astype(jnp.float32)).astype(jnp.bfloat16)


def listed(place, values):
    found = jnp.zeros_like(place)
    for index, value in enumerate(values):
        found = jnp.where(place == index, value, found)
    return found


def dot(left, right):
    return jnp.dot(left, right, preferred_element_type=jnp.float32)


def pack_kernel(
    owners, block, scale, order, last_order, spectra_ref, bin_ref, valid_ref, stack_ref, *refs
):
    pack_ref, held_ref, *tables, bins, valids, sems = refs
    stations = owners * block
    pairs = bins.shape[1]
    lanes = pack_ref.shape[3]
    copies = [
        pltpu.make_async_copy(bin_ref, bins, sems.at[0]),
        pltpu.make_async_copy(valid_ref, valids, sems.at[1]),
        pltpu.make_async_copy(stack_ref, held_ref, sems.at[2]),
    ]
    tiles = pack_ref.shape[1] - stations // lanes * (block // 2)
    if len(spectra_ref.shape) == 3:
        halves = tiles // block
        for place in range(owners * halves):
            slot, half = place // halves, place % halves
            source = spectra_ref.at[:, :, pl.ds((order[slot] * halves + half) * lanes, lanes)]
            target = pack_ref.at[slot, pl.ds(half * block, block)]
            copies.append(pltpu.make_async_copy(source, target, sems.at[3 + place]))
    else:
        for slot in range(owners):
            target = pack_ref.at[slot, pl.ds(0, tiles)]
            copies.append(pltpu.make_async_copy(spectra_ref.at[order[slot]], target, sems.at[3 + slot]))
    for copy in copies:
        copy.start()
    place = iota((block, pairs), 1)
    mine = lax.rem(lax.div(place, block), block) == iota((block, pairs), 0)
    place = iota((pairs, stations), 0)
    ahead = lax.axis_index("stn") + (owners - 1)
    other = lax.rem(ahead - lax.div(place, block * block), owners) * block + lax.rem(place, block)
    column = iota((1, stations), 1)
    column = listed(lax.div(column, block), order) * block + lax.rem(column, block)
    right = jnp.where(other == column, 1.0, 0.0).astype(jnp.bfloat16)
    fill_tables(last_order, scale, *tables)
    copies[0].wait()
    copies[1].wait()
    codes = jnp.where(valids[...] != 0, bins[...] + 1, 0).astype(jnp.float32)
    left = jnp.where(mine, jnp.broadcast_to(codes, (block, pairs)), 0.0).astype(jnp.bfloat16)
    codes = dot(left, right)
    for place in range(stations // lanes):
        piece = codes[:, place * lanes : (place + 1) * lanes].reshape(block // 2, 2, lanes)
        piece = piece.astype(jnp.bfloat16)
        start = tiles + place * (block // 2)
        for owner in range(owners):
            pack_ref[owner, start : start + block // 2] = piece
    for copy in copies[2:]:
        copy.wait()


def bin_kernel(owners, block, halves, last_order, got_ref, sums_ref, rows_ref):
    stations = owners * block
    lanes = got_ref.shape[2]
    start = 2 * halves * block
    codes = [
        got_ref[:, start + place * block : start + (place + 1) * block, :].reshape(stations, lanes)
        for place in range(stations // lanes)
    ]
    codes = jnp.concatenate(codes, axis=1).astype(jnp.float32)
    shape = (lanes, lanes)
    same = lax.div(iota(shape, 0), WBLK) == lax.div(iota(shape, 1), WBLK)
    same = jnp.where(same, 0.5 / WBLK, 0.0).astype(jnp.bfloat16)
    pieces = []
    for half in range(halves):
        raw = got_ref[:, 2 * half * block : 2 * (half + 1) * block, :].astype(jnp.float32)
        rows_ref[half] = raw.reshape(2 * stations, lanes)
        raw = [rows_ref[half, pl.ds(part, stations, stride=2), :] for part in range(2)]
        upper, lower = split(raw[0] * raw[0] + raw[1] * raw[1])
        scale = lax.rsqrt(dot(upper, same) + dot(lower, same) + 1e-06)
        pieces += [(value * scale).astype(jnp.bfloat16) for value in raw]
    right = jnp.concatenate(pieces, axis=1)
    left = [piece.astype(jnp.float32) for piece in pieces]
    for owner in range(owners):
        chosen = jnp.where(codes == float(owner + 1), 1.0, 0.0).astype(jnp.bfloat16)
        mixed = dot(chosen, right)
        for half in range(halves):
            own_re, own_im = left[2 * half], left[2 * half + 1]
            mix_re = mixed[:, 2 * half * lanes : (2 * half + 1) * lanes]
            mix_im = mixed[:, (2 * half + 1) * lanes : (2 * half + 2) * lanes]
            real = jnp.sum(own_re * mix_re + own_im * mix_im, axis=0, keepdims=True)
            imag = jnp.sum(own_im * mix_re - own_re * mix_im, axis=0, keepdims=True)
            for place in range(len(last_order)):
                if last_order[place] % owners != owner:
                    continue
                sums_ref[place, half : half + 1, :] = real
                sums_ref[place, halves + half : halves + half + 1, :] = imag


def turn(product, period, ahead=0.0):
    angle = lax.rem(product, jnp.int32(period)).astype(jnp.float32) * (2.0 * math.pi / period) + ahead
    return jnp.cos(angle), jnp.sin(angle)


def powers(factor, period, count, store, ahead=0.0):
    width = factor.shape[1]
    near_cos, near_sin = turn(factor * iota((TILE, width), 0), period, ahead)
    far_cos, far_sin = turn(factor * (TILE * iota((count // TILE, width), 0)), period)
    for step in range(count // TILE):
        cos, sin = far_cos[step : step + 1, :], far_sin[step : step + 1, :]
        store(step * TILE, near_cos * cos - near_sin * sin, near_sin * cos + near_cos * sin)


def fill_tables(last_order, scale, first_ref, turn_ref, last_ref):
    coarse, span = first_ref.shape[0] // 2, first_ref.shape[1] // 3
    turns, fine = last_ref.shape[0] // 2, last_ref.shape[1] // 2

    width, sources = max(span, LANES), len(last_order)
    column = lax.rem(iota((1, width), 1), span)
    factor = listed(lax.rem(column, sources), last_order)
    ahead = jnp.where(column < sources, 0.0, 0.5 * math.pi)

    def store_first(start, cos, sin):
        for begin, value in ((start, cos), (coarse + start, sin)):
            upper, lower = split(value)
            for place in range(0, 2 * span, width):
                first_ref[begin : begin + TILE, place : place + width] = upper
            first_ref[begin : begin + TILE, 2 * span :] = lower[:, :span]

    def store_turn(start, cos, sin):
        turn_ref[start : start + TILE, :] = cos
        turn_ref[coarse + start : coarse + start + TILE, :] = sin

    powers(factor, coarse, coarse, store_first, ahead)
    powers(iota((1, fine), 1) + 1, SAMPLES, coarse, store_turn)
    shape = (turns, fine)
    band = lax.axis_index("frq")
    bands = lax.axis_size("frq")
    step = iota(shape, 0) + band * turns + (SAMPLES - bands * turns // 2)
    cos, sin = turn((iota(shape, 1) + 1) * step, fine)
    upper, lower = split(jnp.concatenate([cos, -sin], axis=1) * scale)
    last_ref[...] = jnp.concatenate([upper, lower], axis=0)


def lag_kernel(halves, first_ref, turn_ref, last_ref, sums_ref, stack_ref, out_ref):
    coarse = first_ref.shape[0] // 2
    turns = last_ref.shape[0] // 2
    part = lambda row: sums_ref[:, row, :]
    real = jnp.concatenate([part(half) for half in range(halves)], axis=1)
    imag = jnp.concatenate([part(halves + half) for half in range(halves)], axis=1)
    upper, lower = split(jnp.concatenate([real, imag], axis=0))
    mixed = dot(first_ref[...], jnp.concatenate([upper, lower, upper], axis=0))
    mix_re, mix_im = mixed[:coarse], mixed[coarse:]
    cos, sin = turn_ref[:coarse, :], turn_ref[coarse:, :]
    turned = jnp.concatenate([mix_re * cos - mix_im * sin, mix_re * sin + mix_im * cos], axis=1)
    upper, lower = split(turned)
    across = lambda left, right: lax.dot_general(
        left, right, (((1,), (1,)), ((), ())), preferred_element_type=jnp.float32
    )
    lags = across(last_ref[...], upper)
    lags = lags[:turns] + lags[turns:] + across(last_ref[:turns, :], lower)
    for row in range(turns):
        place = slice(row * coarse, (row + 1) * coarse)
        out_ref[:, place] = stack_ref[:, place] + lags[row : row + 1, :]


def orders(owners, bands):
    part = owners // 4
    within = range(part - 1, -1, -1)
    order = [outer * part + inner for outer in (1, 0, 2, 3) for inner in within]
    last = [(band, outer) for outer in range(4) for band in range(bands)]
    return order, [band * owners + outer * part + inner for band, outer in last for inner in within]


def whole(memory=pltpu.VMEM):
    return pl.BlockSpec(memory_space=memory)


def near(value):
    return pltpu.with_memory_space_constraint(value, pltpu.VMEM)


def local(spectra, pair_bin, pair_valid, stack_in):
    block, _, width = spectra.shape
    owners, bands = lax.axis_size("stn"), lax.axis_size("frq")
    stations = owners * block
    pairs = pair_valid.shape[0]
    fine = width // owners
    lanes = min(fine, LANES)
    halves = fine // lanes
    coarse = SAMPLES // fine
    turns = stack_in.shape[1] // coarse
    order, last_order = orders(owners, bands)
    if lanes < LANES:
        spectra = spectra.reshape(block, 2, owners, halves, lanes).transpose(2, 3, 0, 1, 4)
        spectra = spectra.reshape(owners, halves * block, 2, lanes)
    rows = halves * block + stations // lanes * (block // 2)
    packed, stack, *tables = pl.pallas_call(
        functools.partial(pack_kernel, owners, block, 1.0 / (width * bands), order, last_order),
        out_shape=[
            pltpu.VMEM((owners, rows, 2, lanes), jnp.bfloat16),
            pltpu.VMEM(stack_in.shape, jnp.float32),
            pltpu.VMEM((2 * coarse, 6 * owners * bands), jnp.bfloat16),
            pltpu.VMEM((2 * coarse, fine), jnp.float32),
            pltpu.VMEM((2 * turns, 2 * fine), jnp.bfloat16),
        ],
        in_specs=[whole(pl.ANY)] * 4,
        out_specs=[whole()] * 5,
        scratch_shapes=[
            pltpu.VMEM((1, pairs), jnp.int32),
            pltpu.VMEM((1, pairs), jnp.int32),
            pltpu.SemaphoreType.DMA((3 + owners * halves,)),
        ],
    )(spectra, pair_bin.reshape(1, pairs), pair_valid.reshape(1, pairs), stack_in)
    packed = packed.reshape(owners, 2 * rows, lanes)
    got = lax.all_to_all(packed, "stn", 0, 0, axis_index_groups=[order], tiled=True)
    sums = pl.pallas_call(
        functools.partial(bin_kernel, owners, block, halves, last_order),
        out_shape=pltpu.VMEM((owners * bands, 2 * halves, lanes), jnp.float32),
        in_specs=[whole()],
        out_specs=whole(),
        scratch_shapes=[pltpu.VMEM((halves, 2 * stations, lanes), jnp.float32)],
    )(near(got))
    axes = ("frq", "stn")
    sums = lax.all_to_all(sums, axes, 0, 0, axis_index_groups=[last_order], tiled=True)
    return pl.pallas_call(
        functools.partial(lag_kernel, halves),
        out_shape=jax.ShapeDtypeStruct(stack_in.shape, jnp.float32),
        in_specs=[whole()] * 5,
        out_specs=whole(),
    )(*[near(value) for value in (*tables, sums, stack)])


def solution(mesh):
    placed = (P("stn", None, "frq"), P("stn", None), P("stn"), P("stn", "frq"))
    return jax.shard_map(
        local, mesh=mesh, in_specs=placed, out_specs=P("stn", "frq"), check_vma=False
    )
```

```python
import functools
import math

import jax
import jax.numpy as jnp
from jax import lax
from jax.experimental import pallas as pl
from jax.experimental.pallas import tpu as pltpu
from jax.sharding import PartitionSpec as P

ROUNDS = 4
SAMPLES = 32768
WBLK = 32
LANES = 128
TILE = 8


def iota(shape, dimension):
    return lax.broadcasted_iota(jnp.int32, shape, dimension)


def split(value):
    upper = value.astype(jnp.bfloat16)
    return upper, (value - upper.astype(jnp.float32)).astype(jnp.bfloat16)


def listed(place, values):
    found = jnp.zeros_like(place)
    for index, value in enumerate(values):
        found = jnp.where(place == index, value, found)
    return found


def dot(left, right):
    return jnp.dot(left, right, preferred_element_type=jnp.float32)


def pack_kernel(
    owners, block, scale, order, last_order, spectra_ref, bin_ref, valid_ref, stack_ref, *refs
):
    pack_ref, held_ref, *tables, bins, valids, sems = refs
    pairs = bins.shape[1]
    lanes = pack_ref.shape[3]
    copies = [
        pltpu.make_async_copy(bin_ref, bins, sems.at[0]),
        pltpu.make_async_copy(valid_ref, valids, sems.at[1]),
        pltpu.make_async_copy(stack_ref, held_ref, sems.at[2]),
    ]
    rows = pairs // lanes
    tiles = pack_ref.shape[1] - rows // 2
    if len(spectra_ref.shape) == 3:
        halves = tiles // block
        for place in range(owners * halves):
            slot, half = place // halves, place % halves
            source = spectra_ref.at[:, :, pl.ds((order[slot] * halves + half) * lanes, lanes)]
            target = pack_ref.at[slot, pl.ds(half * block, block)]
            copies.append(pltpu.make_async_copy(source, target, sems.at[3 + place]))
    else:
        for slot in range(owners):
            target = pack_ref.at[slot, pl.ds(0, tiles)]
            copies.append(pltpu.make_async_copy(spectra_ref.at[order[slot]], target, sems.at[3 + slot]))
    for copy in copies:
        copy.start()
    reach = ROUNDS * block
    place = iota((TILE, pairs), 1)
    row = lax.div(lax.rem(lax.div(place, block), block), lanes // reach)
    mine = row == iota((TILE, pairs), 0)
    place = iota((pairs, lanes), 0)
    ahead = lax.axis_index("stn") + (owners - 1)
    other = lax.rem(ahead - lax.div(place, block * block), owners)
    station = lax.rem(lax.div(place, block), block)
    column = lax.rem(station, lanes // reach) * reach + lax.rem(other, ROUNDS) * block
    right = column + lax.rem(place, block) == iota((pairs, lanes), 1)
    right = jnp.where(right, 1.0, 0.0).astype(jnp.bfloat16)
    fill_tables(last_order, scale, *tables)
    copies[0].wait()
    copies[1].wait()
    codes = jnp.where(valids[...] != 0, bins[...] + 1, 0).astype(jnp.float32)
    left = jnp.where(mine, jnp.broadcast_to(codes, (TILE, pairs)), 0.0).astype(jnp.bfloat16)
    codes = dot(left, right)[:rows].reshape(rows // 2, 2, lanes).astype(jnp.bfloat16)
    for slot in range(owners):
        pack_ref[slot, tiles:] = codes
    for copy in copies[2:]:
        copy.wait()


def code_grid(order, block, slab, start, rows_ref):
    owners, lanes = len(order), rows_ref.shape[1]
    stations, reach = owners * block, ROUNDS * block
    shape = (block, lanes)
    span = lanes // reach
    row, place = iota(shape, 0), iota(shape, 1)
    seen = lax.rem(row, span) == lax.div(place, reach)
    seen = [seen & (lax.div(row, span) == part) for part in range(block // span)]
    lines = []
    for slot in range(owners):
        line = jnp.zeros(shape, jnp.float32)
        for part, chosen in enumerate(seen):
            place = slot * slab + start + part
            line = jnp.where(chosen, jnp.broadcast_to(rows_ref[place : place + 1, :], shape), line)
        lines.append(line)
    lines = jnp.concatenate(lines, axis=0).astype(jnp.bfloat16)
    shape = (lanes, stations)
    device = listed(lax.div(iota((1, stations), 1), block), order)
    column = lax.rem(device, ROUNDS) * block + lax.rem(iota((1, stations), 1), block)
    spread = jnp.where(lax.rem(iota(shape, 0), reach) == column, 1.0, 0.0).astype(jnp.bfloat16)
    codes = dot(lines, spread)
    device = jnp.broadcast_to(device, (block, stations))
    lines = []
    for slot in range(owners):
        apart = order[slot] - 1 - device
        paired = ((apart >= 0) & (apart < ROUNDS)) | (apart < ROUNDS - owners)
        lines.append(jnp.where(paired, codes[slot * block : (slot + 1) * block], 0.0))
    return jnp.concatenate(lines, axis=0)


def bin_kernel(block, halves, order, last_order, got_ref, sums_ref, rows_ref):
    owners, lanes = len(order), got_ref.shape[1]
    slab, start = got_ref.shape[0] // owners, 2 * halves * block
    rows_ref[...] = got_ref[...].astype(jnp.float32)
    codes = code_grid(order, block, slab, start, rows_ref)
    shape = (lanes, lanes)
    same = lax.div(iota(shape, 0), WBLK) == lax.div(iota(shape, 1), WBLK)
    same = jnp.where(same, 0.5 / WBLK, 0.0).astype(jnp.bfloat16)
    pieces = []
    for half in range(halves):
        raw = []
        for part in range(2):
            first = 2 * half * block + part
            lines = [
                rows_ref[pl.ds(slot * slab + first, block, stride=2), :] for slot in range(owners)
            ]
            raw.append(jnp.concatenate(lines, axis=0))
        upper, lower = split(raw[0] * raw[0] + raw[1] * raw[1])
        scale = lax.rsqrt(dot(upper, same) + dot(lower, same) + 1e-06)
        pieces += [(value * scale).astype(jnp.bfloat16) for value in raw]
    right = jnp.concatenate(pieces, axis=1)
    left = [piece.astype(jnp.float32) for piece in pieces]
    for owner in range(owners):
        chosen = jnp.where(codes == float(owner + 1), 1.0, 0.0).astype(jnp.bfloat16)
        mixed = dot(chosen, right)
        for half in range(halves):
            own_re, own_im = left[2 * half], left[2 * half + 1]
            mix_re = mixed[:, 2 * half * lanes : (2 * half + 1) * lanes]
            mix_im = mixed[:, (2 * half + 1) * lanes : (2 * half + 2) * lanes]
            real = jnp.sum(own_re * mix_re + own_im * mix_im, axis=0, keepdims=True)
            imag = jnp.sum(own_im * mix_re - own_re * mix_im, axis=0, keepdims=True)
            for place in range(len(last_order)):
                if last_order[place] % owners != owner:
                    continue
                sums_ref[place, half : half + 1, :] = real
                sums_ref[place, halves + half : halves + half + 1, :] = imag


def turn(product, period, ahead=0.0):
    angle = lax.rem(product, jnp.int32(period)).astype(jnp.float32) * (2.0 * math.pi / period) + ahead
    return jnp.cos(angle), jnp.sin(angle)


def powers(factor, period, count, store, ahead=0.0):
    width = factor.shape[1]
    near_cos, near_sin = turn(factor * iota((TILE, width), 0), period, ahead)
    far_cos, far_sin = turn(factor * (TILE * iota((count // TILE, width), 0)), period)
    for step in range(count // TILE):
        cos, sin = far_cos[step : step + 1, :], far_sin[step : step + 1, :]
        store(step * TILE, near_cos * cos - near_sin * sin, near_sin * cos + near_cos * sin)


def fill_tables(last_order, scale, first_ref, turn_ref, last_ref):
    coarse, span = first_ref.shape[0] // 2, first_ref.shape[1] // 3
    turns, fine = last_ref.shape[0] // 2, last_ref.shape[1] // 2

    width, sources = max(span, LANES), len(last_order)
    column = lax.rem(iota((1, width), 1), span)
    factor = listed(lax.rem(column, sources), last_order)
    ahead = jnp.where(column < sources, 0.0, 0.5 * math.pi)

    def store_first(start, cos, sin):
        for begin, value in ((start, cos), (coarse + start, sin)):
            upper, lower = split(value)
            for place in range(0, 2 * span, width):
                first_ref[begin : begin + TILE, place : place + width] = upper
            first_ref[begin : begin + TILE, 2 * span :] = lower[:, :span]

    def store_turn(start, cos, sin):
        turn_ref[start : start + TILE, :] = cos
        turn_ref[coarse + start : coarse + start + TILE, :] = sin

    powers(factor, coarse, coarse, store_first, ahead)
    powers(iota((1, fine), 1) + 1, SAMPLES, coarse, store_turn)
    shape = (turns, fine)
    band = lax.axis_index("frq")
    bands = lax.axis_size("frq")
    step = iota(shape, 0) + band * turns + (SAMPLES - bands * turns // 2)
    cos, sin = turn((iota(shape, 1) + 1) * step, fine)
    upper, lower = split(jnp.concatenate([cos, -sin], axis=1) * scale)
    last_ref[...] = jnp.concatenate([upper, lower], axis=0)


def lag_kernel(halves, first_ref, turn_ref, last_ref, sums_ref, stack_ref, out_ref):
    coarse = first_ref.shape[0] // 2
    turns = last_ref.shape[0] // 2
    part = lambda row: sums_ref[:, row, :]
    real = jnp.concatenate([part(half) for half in range(halves)], axis=1)
    imag = jnp.concatenate([part(halves + half) for half in range(halves)], axis=1)
    upper, lower = split(jnp.concatenate([real, imag], axis=0))
    mixed = dot(first_ref[...], jnp.concatenate([upper, lower, upper], axis=0))
    mix_re, mix_im = mixed[:coarse], mixed[coarse:]
    cos, sin = turn_ref[:coarse, :], turn_ref[coarse:, :]
    turned = jnp.concatenate([mix_re * cos - mix_im * sin, mix_re * sin + mix_im * cos], axis=1)
    upper, lower = split(turned)
    across = lambda left, right: lax.dot_general(
        left, right, (((1,), (1,)), ((), ())), preferred_element_type=jnp.float32
    )
    lags = across(last_ref[...], upper)
    lags = lags[:turns] + lags[turns:] + across(last_ref[:turns, :], lower)
    for row in range(turns):
        place = slice(row * coarse, (row + 1) * coarse)
        out_ref[:, place] = stack_ref[:, place] + lags[row : row + 1, :]


def orders(owners, bands):
    part = owners // 4
    within = range(part - 1, -1, -1)
    order = [outer * part + inner for outer in (1, 0, 2, 3) for inner in within]
    last = [(band, outer) for outer in range(4) for band in range(bands)]
    return order, [band * owners + outer * part + inner for band, outer in last for inner in within]


def whole(memory=pltpu.VMEM):
    return pl.BlockSpec(memory_space=memory)


def near(value):
    return pltpu.with_memory_space_constraint(value, pltpu.VMEM)


def local(spectra, pair_bin, pair_valid, stack_in):
    block, _, width = spectra.shape
    owners, bands = lax.axis_size("stn"), lax.axis_size("frq")
    pairs = pair_valid.shape[0]
    fine = width // owners
    lanes = min(fine, LANES)
    halves = fine // lanes
    coarse = SAMPLES // fine
    turns = stack_in.shape[1] // coarse
    order, last_order = orders(owners, bands)
    if lanes < LANES:
        spectra = spectra.reshape(block, 2, owners, halves, lanes).transpose(2, 3, 0, 1, 4)
        spectra = spectra.reshape(owners, halves * block, 2, lanes)
    slab = 2 * halves * block + pairs // lanes
    packed, stack, *tables = pl.pallas_call(
        functools.partial(pack_kernel, owners, block, 1.0 / (width * bands), order, last_order),
        out_shape=[
            pltpu.VMEM((owners, slab // 2, 2, lanes), jnp.bfloat16),
            pltpu.VMEM(stack_in.shape, jnp.float32),
            pltpu.VMEM((2 * coarse, 6 * owners * bands), jnp.bfloat16),
            pltpu.VMEM((2 * coarse, fine), jnp.float32),
            pltpu.VMEM((2 * turns, 2 * fine), jnp.bfloat16),
        ],
        in_specs=[whole(pl.ANY)] * 4,
        out_specs=[whole()] * 5,
        scratch_shapes=[
            pltpu.VMEM((1, pairs), jnp.int32),
            pltpu.VMEM((1, pairs), jnp.int32),
            pltpu.SemaphoreType.DMA((3 + owners * halves,)),
        ],
    )(spectra, pair_bin.reshape(1, pairs), pair_valid.reshape(1, pairs), stack_in)
    got = lax.all_to_all(packed, "stn", 0, 0, axis_index_groups=[order], tiled=True)
    got = got.reshape(owners * slab, lanes)
    sums = pl.pallas_call(
        functools.partial(bin_kernel, block, halves, order, last_order),
        out_shape=pltpu.VMEM((owners * bands, 2 * halves, lanes), jnp.float32),
        in_specs=[whole()],
        out_specs=whole(),
        scratch_shapes=[pltpu.VMEM((owners * slab, lanes), jnp.float32)],
    )(near(got))
    axes = ("frq", "stn")
    sums = lax.all_to_all(sums, axes, 0, 0, axis_index_groups=[last_order], tiled=True)
    return pl.pallas_call(
        functools.partial(lag_kernel, halves),
        out_shape=jax.ShapeDtypeStruct(stack_in.shape, jnp.float32),
        in_specs=[whole()] * 5,
        out_specs=whole(),
    )(*[near(value) for value in (*tables, sums, stack)])


def solution(mesh):
    placed = (P("stn", None, "frq"), P("stn", None), P("stn"), P("stn", "frq"))
    return jax.shard_map(
        local, mesh=mesh, in_specs=placed, out_specs=P("stn", "frq"), check_vma=False
    )
```

```python
import functools
import math

import jax
import jax.numpy as jnp
from jax import lax
from jax.experimental import pallas as pl
from jax.experimental.pallas import tpu as pltpu
from jax.sharding import PartitionSpec as P

ROUNDS = 4
SAMPLES = 32768
WBLK = 32
LANES = 128
TILE = 8


def iota(shape, dimension):
    return lax.broadcasted_iota(jnp.int32, shape, dimension)


def split(value):
    upper = value.astype(jnp.bfloat16)
    return upper, (value - upper.astype(jnp.float32)).astype(jnp.bfloat16)


def listed(place, values):
    found = jnp.zeros_like(place)
    for index, value in enumerate(values):
        found = jnp.where(place == index, value, found)
    return found


def dot(left, right):
    return jnp.dot(left, right, preferred_element_type=jnp.float32)


def pack_kernel(
    owners, block, scale, order, last_order, spectra_ref, bin_ref, valid_ref, stack_ref, *refs
):
    pack_ref, held_ref, *tables, bins, valids, sems = refs
    pairs = bins.shape[1]
    lanes = pack_ref.shape[3]
    copies = [
        pltpu.make_async_copy(bin_ref, bins, sems.at[0]),
        pltpu.make_async_copy(valid_ref, valids, sems.at[1]),
        pltpu.make_async_copy(stack_ref, held_ref, sems.at[2]),
    ]
    rows = pairs // lanes
    tiles = pack_ref.shape[1] - rows // 2
    if len(spectra_ref.shape) == 3:
        halves = tiles // block
        for place in range(owners * halves):
            slot, half = place // halves, place % halves
            source = spectra_ref.at[:, :, pl.ds((order[slot] * halves + half) * lanes, lanes)]
            target = pack_ref.at[slot, pl.ds(half * block, block)]
            copies.append(pltpu.make_async_copy(source, target, sems.at[3 + place]))
    else:
        for slot in range(owners):
            target = pack_ref.at[slot, pl.ds(0, tiles)]
            copies.append(pltpu.make_async_copy(spectra_ref.at[order[slot]], target, sems.at[3 + slot]))
    for copy in copies:
        copy.start()
    reach = ROUNDS * block
    place = iota((TILE, pairs), 1)
    row = lax.div(lax.rem(lax.div(place, block), block), lanes // reach)
    mine = row == iota((TILE, pairs), 0)
    place = iota((pairs, lanes), 0)
    ahead = lax.axis_index("stn") + (owners - 1)
    other = lax.rem(ahead - lax.div(place, block * block), owners)
    station = lax.rem(lax.div(place, block), block)
    column = lax.rem(station, lanes // reach) * reach + lax.rem(other, ROUNDS) * block
    right = column + lax.rem(place, block) == iota((pairs, lanes), 1)
    right = jnp.where(right, 1.0, 0.0).astype(jnp.bfloat16)
    fill_tables(last_order, scale, *tables)
    copies[0].wait()
    copies[1].wait()
    codes = jnp.where(valids[...] != 0, bins[...] + 1, 0).astype(jnp.float32)
    left = jnp.where(mine, jnp.broadcast_to(codes, (TILE, pairs)), 0.0).astype(jnp.bfloat16)
    codes = dot(left, right)[:rows].reshape(rows // 2, 2, lanes).astype(jnp.bfloat16)
    for slot in range(owners):
        pack_ref[slot, tiles:] = codes
    for copy in copies[2:]:
        copy.wait()


def code_grid(order, block, slab, start, rows_ref):
    owners, lanes = len(order), rows_ref.shape[1]
    stations, reach = owners * block, ROUNDS * block
    shape = (block, lanes)
    span = lanes // reach
    row, place = iota(shape, 0), iota(shape, 1)
    seen = lax.rem(row, span) == lax.div(place, reach)
    seen = [seen & (lax.div(row, span) == part) for part in range(block // span)]
    lines = []
    for slot in range(owners):
        line = jnp.zeros(shape, jnp.float32)
        for part, chosen in enumerate(seen):
            place = slot * slab + start + part
            line = jnp.where(chosen, jnp.broadcast_to(rows_ref[place : place + 1, :], shape), line)
        lines.append(line)
    lines = jnp.concatenate(lines, axis=0).astype(jnp.bfloat16)
    shape = (lanes, stations)
    device = listed(lax.div(iota((1, stations), 1), block), order)
    column = lax.rem(device, ROUNDS) * block + lax.rem(iota((1, stations), 1), block)
    spread = jnp.where(lax.rem(iota(shape, 0), reach) == column, 1.0, 0.0).astype(jnp.bfloat16)
    codes = dot(lines, spread)
    device = jnp.broadcast_to(device, (block, stations))
    lines = []
    for slot in range(owners):
        apart = order[slot] - 1 - device
        paired = ((apart >= 0) & (apart < ROUNDS)) | (apart < ROUNDS - owners)
        lines.append(jnp.where(paired, codes[slot * block : (slot + 1) * block], 0.0))
    return jnp.concatenate(lines, axis=0)


def bin_kernel(block, halves, order, last_order, got_ref, sums_ref, rows_ref):
    owners, lanes = len(order), got_ref.shape[1]
    slab, start = got_ref.shape[0] // owners, 2 * halves * block
    rows_ref[...] = got_ref[...].astype(jnp.float32)
    codes = code_grid(order, block, slab, start, rows_ref).astype(jnp.bfloat16)
    one, zero = jnp.ones((), jnp.bfloat16), jnp.zeros((), jnp.bfloat16)
    shape = (lanes, lanes)
    same = lax.div(iota(shape, 0), WBLK) == lax.div(iota(shape, 1), WBLK)
    same = jnp.where(same, 0.5 / WBLK, 0.0).astype(jnp.bfloat16)
    pieces = []
    for half in range(halves):
        raw = []
        for part in range(2):
            first = 2 * half * block + part
            lines = [
                rows_ref[pl.ds(slot * slab + first, block, stride=2), :] for slot in range(owners)
            ]
            raw.append(jnp.concatenate(lines, axis=0))
        upper, lower = split(raw[0] * raw[0] + raw[1] * raw[1])
        scale = lax.rsqrt(dot(upper, same) + dot(lower, same) + 1e-06)
        pieces += [(value * scale).astype(jnp.bfloat16) for value in raw]
    right = jnp.concatenate(pieces, axis=1)
    left = [piece.astype(jnp.float32) for piece in pieces]
    for owner in range(owners):
        chosen = jnp.where(codes == jnp.bfloat16(owner + 1), one, zero)
        mixed = dot(chosen, right)
        for half in range(halves):
            own_re, own_im = left[2 * half], left[2 * half + 1]
            mix_re = mixed[:, 2 * half * lanes : (2 * half + 1) * lanes]
            mix_im = mixed[:, (2 * half + 1) * lanes : (2 * half + 2) * lanes]
            real = jnp.sum(own_re * mix_re + own_im * mix_im, axis=0, keepdims=True)
            imag = jnp.sum(own_im * mix_re - own_re * mix_im, axis=0, keepdims=True)
            for place in range(len(last_order)):
                if last_order[place] % owners != owner:
                    continue
                sums_ref[place, half : half + 1, :] = real
                sums_ref[place, halves + half : halves + half + 1, :] = imag


def turn(product, period, ahead=0.0):
    angle = lax.rem(product, jnp.int32(period)).astype(jnp.float32) * (2.0 * math.pi / period) + ahead
    return jnp.cos(angle), jnp.sin(angle)


def powers(factor, period, count, store, ahead=0.0):
    width = factor.shape[1]
    near_cos, near_sin = turn(factor * iota((TILE, width), 0), period, ahead)
    far_cos, far_sin = turn(factor * (TILE * iota((count // TILE, width), 0)), period)
    for step in range(count // TILE):
        cos, sin = far_cos[step : step + 1, :], far_sin[step : step + 1, :]
        store(step * TILE, near_cos * cos - near_sin * sin, near_sin * cos + near_cos * sin)


def fill_tables(last_order, scale, first_ref, turn_ref, last_ref):
    coarse, span = first_ref.shape[0] // 2, first_ref.shape[1] // 3
    turns, fine = last_ref.shape[0] // 2, last_ref.shape[1] // 2

    width, sources = max(span, LANES), len(last_order)
    column = lax.rem(iota((1, width), 1), span)
    factor = listed(lax.rem(column, sources), last_order)
    ahead = jnp.where(column < sources, 0.0, 0.5 * math.pi)

    def store_first(start, cos, sin):
        for begin, value in ((start, cos), (coarse + start, sin)):
            upper, lower = split(value)
            for place in range(0, 2 * span, width):
                first_ref[begin : begin + TILE, place : place + width] = upper
            first_ref[begin : begin + TILE, 2 * span :] = lower[:, :span]

    def store_turn(start, cos, sin):
        turn_ref[start : start + TILE, :] = cos
        turn_ref[coarse + start : coarse + start + TILE, :] = sin

    powers(factor, coarse, coarse, store_first, ahead)
    powers(iota((1, fine), 1) + 1, SAMPLES, coarse, store_turn)
    shape = (turns, fine)
    band = lax.axis_index("frq")
    bands = lax.axis_size("frq")
    step = iota(shape, 0) + band * turns + (SAMPLES - bands * turns // 2)
    cos, sin = turn((iota(shape, 1) + 1) * step, fine)
    upper, lower = split(jnp.concatenate([cos, -sin], axis=1) * scale)
    last_ref[...] = jnp.concatenate([upper, lower], axis=0)


def lag_kernel(halves, first_ref, turn_ref, last_ref, sums_ref, stack_ref, out_ref):
    coarse = first_ref.shape[0] // 2
    turns = last_ref.shape[0] // 2
    part = lambda row: sums_ref[:, row, :]
    real = jnp.concatenate([part(half) for half in range(halves)], axis=1)
    imag = jnp.concatenate([part(halves + half) for half in range(halves)], axis=1)
    upper, lower = split(jnp.concatenate([real, imag], axis=0))
    mixed = dot(first_ref[...], jnp.concatenate([upper, lower, upper], axis=0))
    mix_re, mix_im = mixed[:coarse], mixed[coarse:]
    cos, sin = turn_ref[:coarse, :], turn_ref[coarse:, :]
    turned = jnp.concatenate([mix_re * cos - mix_im * sin, mix_re * sin + mix_im * cos], axis=1)
    upper, lower = split(turned)
    across = lambda left, right: lax.dot_general(
        left, right, (((1,), (1,)), ((), ())), preferred_element_type=jnp.float32
    )
    lags = across(last_ref[...], upper)
    lags = lags[:turns] + lags[turns:] + across(last_ref[:turns, :], lower)
    for row in range(turns):
        place = slice(row * coarse, (row + 1) * coarse)
        out_ref[:, place] = stack_ref[:, place] + lags[row : row + 1, :]


def orders(owners, bands):
    part = owners // 4
    within = range(part - 1, -1, -1)
    order = [outer * part + inner for outer in (2, 3, 1, 0) for inner in within]
    last = [(band, outer) for outer in range(4) for band in range(bands)]
    return order, [band * owners + outer * part + inner for band, outer in last for inner in within]


def whole(memory=pltpu.VMEM):
    return pl.BlockSpec(memory_space=memory)


def near(value):
    return pltpu.with_memory_space_constraint(value, pltpu.VMEM)


def local(spectra, pair_bin, pair_valid, stack_in):
    block, _, width = spectra.shape
    owners, bands = lax.axis_size("stn"), lax.axis_size("frq")
    pairs = pair_valid.shape[0]
    fine = width // owners
    lanes = min(fine, LANES)
    halves = fine // lanes
    coarse = SAMPLES // fine
    turns = stack_in.shape[1] // coarse
    order, last_order = orders(owners, bands)
    if lanes < LANES:
        spectra = spectra.reshape(block, 2, owners, halves, lanes).transpose(2, 3, 0, 1, 4)
        spectra = spectra.reshape(owners, halves * block, 2, lanes)
    slab = 2 * halves * block + pairs // lanes
    packed, stack, *tables = pl.pallas_call(
        functools.partial(pack_kernel, owners, block, 1.0 / (width * bands), order, last_order),
        out_shape=[
            pltpu.VMEM((owners, slab // 2, 2, lanes), jnp.bfloat16),
            pltpu.VMEM(stack_in.shape, jnp.float32),
            pltpu.VMEM((2 * coarse, 6 * owners * bands), jnp.bfloat16),
            pltpu.VMEM((2 * coarse, fine), jnp.float32),
            pltpu.VMEM((2 * turns, 2 * fine), jnp.bfloat16),
        ],
        in_specs=[whole(pl.ANY)] * 4,
        out_specs=[whole()] * 5,
        scratch_shapes=[
            pltpu.VMEM((1, pairs), jnp.int32),
            pltpu.VMEM((1, pairs), jnp.int32),
            pltpu.SemaphoreType.DMA((3 + owners * halves,)),
        ],
    )(spectra, pair_bin.reshape(1, pairs), pair_valid.reshape(1, pairs), stack_in)
    got = lax.all_to_all(packed, "stn", 0, 0, axis_index_groups=[order], tiled=True)
    got = got.reshape(owners * slab, lanes)
    sums = pl.pallas_call(
        functools.partial(bin_kernel, block, halves, order, last_order),
        out_shape=pltpu.VMEM((owners * bands, 2 * halves, lanes), jnp.float32),
        in_specs=[whole()],
        out_specs=whole(),
        scratch_shapes=[pltpu.VMEM((owners * slab, lanes), jnp.float32)],
    )(near(got))
    axes = ("frq", "stn")
    sums = lax.all_to_all(sums, axes, 0, 0, axis_index_groups=[last_order], tiled=True)
    return pl.pallas_call(
        functools.partial(lag_kernel, halves),
        out_shape=jax.ShapeDtypeStruct(stack_in.shape, jnp.float32),
        in_specs=[whole()] * 5,
        out_specs=whole(),
    )(*[near(value) for value in (*tables, sums, stack)])


def solution(mesh):
    placed = (P("stn", None, "frq"), P("stn", None), P("stn"), P("stn", "frq"))
    return jax.shard_map(
        local, mesh=mesh, in_specs=placed, out_specs=P("stn", "frq"), check_vma=False
    )
```

```python
import functools
import math

import jax
import jax.numpy as jnp
from jax import lax
from jax.experimental import pallas as pl
from jax.experimental.pallas import tpu as pltpu
from jax.sharding import PartitionSpec as P

ROUNDS = 4
SAMPLES = 32768
WBLK = 32
LANES = 128
TILE = 8


def iota(shape, dimension):
    return lax.broadcasted_iota(jnp.int32, shape, dimension)


def split(value):
    upper = value.astype(jnp.bfloat16)
    return upper, (value - upper.astype(jnp.float32)).astype(jnp.bfloat16)


def listed(place, values):
    found = jnp.zeros_like(place)
    for index, value in enumerate(values):
        found = jnp.where(place == index, value, found)
    return found


def dot(left, right):
    return jnp.dot(left, right, preferred_element_type=jnp.float32)


def pack_kernel(
    owners, block, scale, order, last_order, spectra_ref, bin_ref, valid_ref, stack_ref, *refs
):
    pack_ref, held_ref, *tables, bins, valids, sems = refs
    pairs = bins.shape[1]
    lanes = pack_ref.shape[3]
    copies = [
        pltpu.make_async_copy(bin_ref, bins, sems.at[0]),
        pltpu.make_async_copy(valid_ref, valids, sems.at[1]),
        pltpu.make_async_copy(stack_ref, held_ref, sems.at[2]),
    ]
    rows = pairs // lanes
    tiles = pack_ref.shape[1] - rows // 2
    if len(spectra_ref.shape) == 3:
        halves = tiles // block
        for place in range(owners * halves):
            slot, half = place // halves, place % halves
            source = spectra_ref.at[:, :, pl.ds((order[slot] * halves + half) * lanes, lanes)]
            target = pack_ref.at[slot, pl.ds(half * block, block)]
            copies.append(pltpu.make_async_copy(source, target, sems.at[3 + place]))
    else:
        for slot in range(owners):
            target = pack_ref.at[slot, pl.ds(0, tiles)]
            copies.append(pltpu.make_async_copy(spectra_ref.at[order[slot]], target, sems.at[3 + slot]))
    for copy in copies:
        copy.start()
    reach = ROUNDS * block
    place = iota((TILE, pairs), 1)
    row = lax.div(lax.rem(lax.div(place, block), block), lanes // reach)
    mine = row == iota((TILE, pairs), 0)
    place = iota((pairs, lanes), 0)
    ahead = lax.axis_index("stn") + (owners - 1)
    other = lax.rem(ahead - lax.div(place, block * block), owners)
    station = lax.rem(lax.div(place, block), block)
    column = lax.rem(station, lanes // reach) * reach + lax.rem(other, ROUNDS) * block
    right = column + lax.rem(place, block) == iota((pairs, lanes), 1)
    right = jnp.where(right, 1.0, 0.0).astype(jnp.bfloat16)
    fill_tables(last_order, scale, *tables)
    copies[0].wait()
    copies[1].wait()
    codes = jnp.where(valids[...] != 0, bins[...] + 1, 0).astype(jnp.float32)
    left = jnp.where(mine, jnp.broadcast_to(codes, (TILE, pairs)), 0.0).astype(jnp.bfloat16)
    codes = dot(left, right)[:rows].reshape(rows // 2, 2, lanes).astype(jnp.bfloat16)
    for slot in range(owners):
        pack_ref[slot, tiles:] = codes
    for copy in copies[2:]:
        copy.wait()


def code_grid(order, block, slab, start, rows_ref):
    owners, lanes = len(order), rows_ref.shape[1]
    stations, reach = owners * block, ROUNDS * block
    shape = (block, lanes)
    span = lanes // reach
    row, place = iota(shape, 0), iota(shape, 1)
    seen = lax.rem(row, span) == lax.div(place, reach)
    seen = [seen & (lax.div(row, span) == part) for part in range(block // span)]
    lines = []
    for slot in range(owners):
        line = jnp.zeros(shape, jnp.float32)
        for part, chosen in enumerate(seen):
            place = slot * slab + start + part
            line = jnp.where(chosen, jnp.broadcast_to(rows_ref[place : place + 1, :], shape), line)
        lines.append(line)
    lines = jnp.concatenate(lines, axis=0).astype(jnp.bfloat16)
    shape = (lanes, stations)
    device = listed(lax.div(iota((1, stations), 1), block), order)
    column = lax.rem(device, ROUNDS) * block + lax.rem(iota((1, stations), 1), block)
    spread = jnp.where(lax.rem(iota(shape, 0), reach) == column, 1.0, 0.0).astype(jnp.bfloat16)
    codes = dot(lines, spread)
    device = jnp.broadcast_to(device, (block, stations))
    lines = []
    for slot in range(owners):
        apart = order[slot] - 1 - device
        paired = ((apart >= 0) & (apart < ROUNDS)) | (apart < ROUNDS - owners)
        lines.append(jnp.where(paired, codes[slot * block : (slot + 1) * block], 0.0))
    return jnp.concatenate(lines, axis=0)


def bin_kernel(block, halves, order, last_order, got_ref, sums_ref, rows_ref):
    owners, lanes = len(order), got_ref.shape[1]
    slab, start = got_ref.shape[0] // owners, 2 * halves * block
    rows_ref[...] = got_ref[...].astype(jnp.float32)
    codes = code_grid(order, block, slab, start, rows_ref)
    shape = (lanes, lanes)
    same = lax.div(iota(shape, 0), WBLK) == lax.div(iota(shape, 1), WBLK)
    same = jnp.where(same, 0.5 / WBLK, 0.0).astype(jnp.bfloat16)
    pieces = []
    for half in range(halves):
        raw = []
        for part in range(2):
            first = 2 * half * block + part
            lines = [
                rows_ref[pl.ds(slot * slab + first, block, stride=2), :] for slot in range(owners)
            ]
            raw.append(jnp.concatenate(lines, axis=0))
        upper, lower = split(raw[0] * raw[0] + raw[1] * raw[1])
        scale = lax.rsqrt(dot(upper, same) + dot(lower, same) + 1e-06)
        pieces += [(value * scale).astype(jnp.bfloat16) for value in raw]
    right = jnp.concatenate(pieces, axis=1)
    left = [piece.astype(jnp.float32) for piece in pieces]
    for owner in range(owners):
        chosen = jnp.where(codes == float(owner + 1), 1.0, 0.0).astype(jnp.bfloat16)
        mixed = dot(chosen, right)
        for half in range(halves):
            own_re, own_im = left[2 * half], left[2 * half + 1]
            mix_re = mixed[:, 2 * half * lanes : (2 * half + 1) * lanes]
            mix_im = mixed[:, (2 * half + 1) * lanes : (2 * half + 2) * lanes]
            real = jnp.sum(own_re * mix_re + own_im * mix_im, axis=0, keepdims=True)
            imag = jnp.sum(own_im * mix_re - own_re * mix_im, axis=0, keepdims=True)
            for place in range(len(last_order)):
                if last_order[place] % owners != owner:
                    continue
                sums_ref[place, half : half + 1, :] = real.astype(sums_ref.dtype)
                sums_ref[place, halves + half : halves + half + 1, :] = imag.astype(sums_ref.dtype)


def turn(product, period, ahead=0.0):
    angle = lax.rem(product, jnp.int32(period)).astype(jnp.float32) * (2.0 * math.pi / period) + ahead
    return jnp.cos(angle), jnp.sin(angle)


def powers(factor, period, count, store, ahead=0.0):
    width = factor.shape[1]
    near_cos, near_sin = turn(factor * iota((TILE, width), 0), period, ahead)
    far_cos, far_sin = turn(factor * (TILE * iota((count // TILE, width), 0)), period)
    for step in range(count // TILE):
        cos, sin = far_cos[step : step + 1, :], far_sin[step : step + 1, :]
        store(step * TILE, near_cos * cos - near_sin * sin, near_sin * cos + near_cos * sin)


def fill_tables(last_order, scale, first_ref, turn_ref, last_ref):
    coarse, span = first_ref.shape[0] // 2, first_ref.shape[1] // 3
    turns, fine = last_ref.shape[0] // 2, last_ref.shape[1] // 2

    width, sources = max(span, LANES), len(last_order)
    column = lax.rem(iota((1, width), 1), span)
    factor = listed(lax.rem(column, sources), last_order)
    ahead = jnp.where(column < sources, 0.0, 0.5 * math.pi)

    def store_first(start, cos, sin):
        for begin, value in ((start, cos), (coarse + start, sin)):
            upper, lower = split(value)
            for place in range(0, 2 * span, width):
                first_ref[begin : begin + TILE, place : place + width] = upper
            first_ref[begin : begin + TILE, 2 * span :] = lower[:, :span]

    def store_turn(start, cos, sin):
        turn_ref[start : start + TILE, :] = cos
        turn_ref[coarse + start : coarse + start + TILE, :] = sin

    powers(factor, coarse, coarse, store_first, ahead)
    powers(iota((1, fine), 1) + 1, SAMPLES, coarse, store_turn)
    shape = (turns, fine)
    band = lax.axis_index("frq")
    bands = lax.axis_size("frq")
    step = iota(shape, 0) + band * turns + (SAMPLES - bands * turns // 2)
    cos, sin = turn((iota(shape, 1) + 1) * step, fine)
    upper, lower = split(jnp.concatenate([cos, -sin], axis=1) * scale)
    last_ref[...] = jnp.concatenate([upper, lower], axis=0)


def lag_kernel(halves, first_ref, turn_ref, last_ref, sums_ref, stack_ref, out_ref):
    coarse = first_ref.shape[0] // 2
    turns = last_ref.shape[0] // 2
    part = lambda row: sums_ref[:, row, :].astype(jnp.float32)
    real = jnp.concatenate([part(half) for half in range(halves)], axis=1)
    imag = jnp.concatenate([part(halves + half) for half in range(halves)], axis=1)
    upper, lower = split(jnp.concatenate([real, imag], axis=0))
    mixed = dot(first_ref[...], jnp.concatenate([upper, lower, upper], axis=0))
    mix_re, mix_im = mixed[:coarse], mixed[coarse:]
    cos, sin = turn_ref[:coarse, :], turn_ref[coarse:, :]
    turned = jnp.concatenate([mix_re * cos - mix_im * sin, mix_re * sin + mix_im * cos], axis=1)
    upper, lower = split(turned)
    across = lambda left, right: lax.dot_general(
        left, right, (((1,), (1,)), ((), ())), preferred_element_type=jnp.float32
    )
    lags = across(last_ref[...], upper)
    lags = lags[:turns] + lags[turns:] + across(last_ref[:turns, :], lower)
    for row in range(turns):
        place = slice(row * coarse, (row + 1) * coarse)
        out_ref[:, place] = stack_ref[:, place] + lags[row : row + 1, :]


def orders(owners, bands):
    part = owners // 4
    within = range(part - 1, -1, -1)
    order = [outer * part + inner for outer in (1, 0, 2, 3) for inner in within]
    last = [(band, outer) for outer in range(4) for band in range(bands)]
    return order, [band * owners + outer * part + inner for band, outer in last for inner in within]


def whole(memory=pltpu.VMEM):
    return pl.BlockSpec(memory_space=memory)


def near(value):
    return pltpu.with_memory_space_constraint(value, pltpu.VMEM)


def local(spectra, pair_bin, pair_valid, stack_in):
    block, _, width = spectra.shape
    owners, bands = lax.axis_size("stn"), lax.axis_size("frq")
    pairs = pair_valid.shape[0]
    fine = width // owners
    lanes = min(fine, LANES)
    halves = fine // lanes
    coarse = SAMPLES // fine
    turns = stack_in.shape[1] // coarse
    order, last_order = orders(owners, bands)
    if lanes < LANES:
        spectra = spectra.reshape(block, 2, owners, halves, lanes).transpose(2, 3, 0, 1, 4)
        spectra = spectra.reshape(owners, halves * block, 2, lanes)
    slab = 2 * halves * block + pairs // lanes
    packed, stack, *tables = pl.pallas_call(
        functools.partial(pack_kernel, owners, block, 1.0 / (width * bands), order, last_order),
        out_shape=[
            pltpu.VMEM((owners, slab // 2, 2, lanes), jnp.bfloat16),
            pltpu.VMEM(stack_in.shape, jnp.float32),
            pltpu.VMEM((2 * coarse, 6 * owners * bands), jnp.bfloat16),
            pltpu.VMEM((2 * coarse, fine), jnp.float32),
            pltpu.VMEM((2 * turns, 2 * fine), jnp.bfloat16),
        ],
        in_specs=[whole(pl.ANY)] * 4,
        out_specs=[whole()] * 5,
        scratch_shapes=[
            pltpu.VMEM((1, pairs), jnp.int32),
            pltpu.VMEM((1, pairs), jnp.int32),
            pltpu.SemaphoreType.DMA((3 + owners * halves,)),
        ],
    )(spectra, pair_bin.reshape(1, pairs), pair_valid.reshape(1, pairs), stack_in)
    got = lax.all_to_all(packed, "stn", 0, 0, axis_index_groups=[order], tiled=True)
    got = got.reshape(owners * slab, lanes)
    sums = pl.pallas_call(
        functools.partial(bin_kernel, block, halves, order, last_order),
        out_shape=pltpu.VMEM((owners * bands, 2 * halves, lanes), jnp.bfloat16),
        in_specs=[whole()],
        out_specs=whole(),
        scratch_shapes=[pltpu.VMEM((owners * slab, lanes), jnp.float32)],
    )(near(got))
    axes = ("frq", "stn")
    sums = lax.all_to_all(sums, axes, 0, 0, axis_index_groups=[last_order], tiled=True)
    return pl.pallas_call(
        functools.partial(lag_kernel, halves),
        out_shape=jax.ShapeDtypeStruct(stack_in.shape, jnp.float32),
        in_specs=[whole()] * 5,
        out_specs=whole(),
    )(*[near(value) for value in (*tables, sums, stack)])


def solution(mesh):
    placed = (P("stn", None, "frq"), P("stn", None), P("stn"), P("stn", "frq"))
    return jax.shard_map(
        local, mesh=mesh, in_specs=placed, out_specs=P("stn", "frq"), check_vma=False
    )
```
